32 devices in a mesh: rows: 8 (over z, y), rhs: 4 (over x, core).
Axes of the slice: x: 2, y: 2, z: 4, core: 2. Of those that a mesh axis runs over, the one named last changes fastest.
Arguments:
- right_sides: bfloat16 [65536, 1024], P(None, ('rows', 'rhs')), may hold values from -6 to 6
- col_panels: bfloat16 [2, 65536, 1024], P(None, ('rows', 'rhs')), may hold values from -0.1875 to 0.1875
- diag_inverses: bfloat16 [2, 1024, 1024], replicated, may hold values from -0.1875 to 0.1875
Outputs:
- current: float32 [65536, 1024], P(('rows', 'rhs'))
The draws below stay inside these ranges and needn't reach their ends.
All inputs are finite; a program needn't handle non-finite values.
Results may differ from the reference program's by a relative error of at most 0.003.
Values may be sent and summed in bfloat16 or wider, within the bound.
No kernel may reach another device: no remote copies, remote signals or barrier semaphores. Data moves between devices by JAX's collectives and lax.ppermute only.
A program may use at most 128 MiB of HBM per device.

```python
import jax
import jax.numpy as jnp
from jax import lax

NB = 1024
M = 1024
PANELS = 2
N = 65536


def block_levels(key, dims, pieces, least, high):
    def one(axis_at, shards_of):
        heights = jax.random.uniform(jax.random.fold_in(jax.random.fold_in(key, 6), axis_at), (shards_of,), jnp.float32, least / len(pieces), high / len(pieces))
        return jnp.repeat(jnp.exp(heights), dims[axis_at] // shards_of).reshape((-1,) + (1,) * (len(dims) - axis_at - 1))

    level = one(*pieces[0])
    for cut in pieces[1:]:
        level = level * one(*cut)
    return level


def gaussian(stream_key, shape, width, limit, cuts=(), kind=jnp.bfloat16):
    values = width * jax.random.normal(stream_key, shape, jnp.float32)
    if cuts:
        values = values * block_levels(stream_key, shape, cuts, -0.22, 0.18)
    return jnp.clip(values, -limit, limit).astype(kind)


def setup_inputs(seed: int = 0) -> dict:
    arg_keys = jax.random.split(jax.random.key(seed), 4)
    return {
        "right_sides": gaussian(arg_keys[0], (N, M), 1.0, 6.0, ((1, 32),)),
        "col_panels": gaussian(arg_keys[1], (PANELS, N, NB), NB ** -0.5, 0.1875, ((1, 32),)),
        "diag_inverses": gaussian(arg_keys[2], (PANELS, NB, NB), NB ** -0.5, 0.1875),
    }


def reference(right_sides, col_panels, diag_inverses):
    current = right_sides.astype(jnp.float32)
    row_count = current.shape[0]
    row_index = jnp.arange(row_count, dtype=jnp.int32)
    for panel_id in range(PANELS):
        first_row = panel_id * (row_count // PANELS)
        panel = current[first_row:first_row + NB].astype(jnp.bfloat16)
        solved = jnp.dot(diag_inverses[panel_id], panel, preferred_element_type=jnp.float32).astype(jnp.bfloat16)
        update_term = jnp.dot(col_panels[panel_id], solved, preferred_element_type=jnp.float32)
        trailing = (row_index >= first_row + NB)[:, None]
        current = jnp.where(trailing, current - update_term, current)
        current = lax.dynamic_update_slice_in_dim(current, solved.astype(jnp.float32), first_row, 0)
    return current
```

```python
import jax
import jax.numpy as jnp
from jax import lax
from jax.experimental import pallas as pl
from jax.experimental.pallas import tpu as pltpu
from jax.sharding import PartitionSpec as P

AXES = ("rows", "rhs")
F32 = jnp.float32
BF16 = jnp.bfloat16


def swap(x, mask, n):
    return lax.ppermute(x, AXES, [(i, i ^ mask) for i in range(n)])


def scatter_block(block, owner, n, me):
    half = n // 2
    piece = block.shape[0] // half
    slots = block.reshape(half // 2, 2, piece, block.shape[1])
    odd = lax.ppermute(slots[:, 1], AXES, [(owner, owner + 1)])
    mine = jnp.where(me == owner, slots[:, 0], odd)
    got = mine[0]
    for t in range(1, half // 2):
        pairs = [(owner, owner + 2 * t), (owner + 1, owner + 1 + 2 * t)]
        here = lax.ppermute(mine[t], AXES, pairs)
        got = jnp.where(me // 2 == owner // 2 + t, here, got)
    return got


def update_kernel(pos_ref, a_ref, c_ref, s0_ref, s1_ref, o_ref, *, owner, panel_blocks):
    i = pl.program_id(0)
    pos = pos_ref[0]
    in_panel = i < panel_blocks
    top0 = jnp.logical_and(pos == 0, in_panel)
    top1 = jnp.logical_and(pos == owner, in_panel)
    tm = o_ref.shape[0]

    @pl.when(jnp.logical_not(jnp.logical_or(top0, top1)))
    def _():
        base = a_ref[...].astype(F32).T
        o_ref[...] = base - jnp.dot(c_ref[0], s0_ref[...], preferred_element_type=F32)

        @pl.when(pos >= owner)
        def _():
            o_ref[...] -= jnp.dot(c_ref[1], s1_ref[...], preferred_element_type=F32)

    start = pl.multiple_of(jnp.where(in_panel, i, 0) * tm, tm)

    @pl.when(top0)
    def _():
        o_ref[...] = s0_ref[pl.ds(start, tm), :].astype(F32)

    @pl.when(top1)
    def _():
        o_ref[...] = s1_ref[pl.ds(start, tm), :].astype(F32)


def update(pos, a_t, cols, s0, s1, owner):
    width, rows = a_t.shape
    nb = s0.shape[0]
    tm = 256
    return pl.pallas_call(
        lambda *refs: update_kernel(*refs, owner=owner, panel_blocks=nb // tm),
        out_shape=jax.ShapeDtypeStruct((rows, width), F32),
        grid_spec=pltpu.PrefetchScalarGridSpec(
            num_scalar_prefetch=1,
            grid=(rows // tm,),
            in_specs=[
                pl.BlockSpec((width, tm), lambda i, p: (0, i)),
                pl.BlockSpec((2, tm, nb), lambda i, p: (0, i, 0)),
                pl.BlockSpec((nb, width), lambda i, p: (0, 0)),
                pl.BlockSpec((nb, width), lambda i, p: (0, 0)),
            ],
            out_specs=pl.BlockSpec((tm, width), lambda i, p: (i, 0)),
        ),
        compiler_params=pltpu.CompilerParams(vmem_limit_bytes=60 << 20),
        cost_estimate=pl.CostEstimate(
            flops=4 * rows * width * nb, bytes_accessed=20 << 20, transcendentals=0
        ),
        name="update",
    )(pos, a_t, cols, s0, s1)


def local(right_sides, col_panels, diag_inverses):
    n = lax.axis_size("rows") * lax.axis_size("rhs")
    me = lax.axis_index(AXES)
    nb = diag_inverses.shape[1]
    total_rows, width = right_sides.shape
    half = n // 2
    owner = half
    x_t = right_sides.T
    pan = jnp.stack([x_t[:, :nb], x_t[:, total_rows // 2 : total_rows // 2 + nb]])
    other = swap(pan, half, n)
    low = jnp.where(me < half, pan, other)
    high = jnp.where(me < half, other, pan)
    piece = scatter_block(col_panels[0, :nb], owner, n, me)
    mine = jnp.concatenate([low[0], high[0], low[1], high[1], piece], axis=0)
    groups = [list(range(half)), list(range(half, n))]
    all_in = lax.all_gather(mine, AXES, axis=0, axis_index_groups=groups)

    a_t = lax.all_to_all(right_sides, AXES, split_axis=0, concat_axis=1, tiled=True).T

    def rows_of(at):
        return all_in[:, at : at + width].reshape(half * width, nb)

    rs0_t = jnp.concatenate([rows_of(0), rows_of(width)], axis=0)
    rs1_t = jnp.concatenate([rows_of(2 * width), rows_of(3 * width)], axis=0)
    block = all_in[:, 4 * width :].reshape(nb, nb)
    nt = (((1,), (1,)), ((), ()))
    s0 = lax.dot_general(diag_inverses[0], rs0_t, nt, preferred_element_type=F32).astype(BF16)
    k0 = jnp.dot(block, s0, preferred_element_type=F32)
    panel1 = (rs1_t.T.astype(F32) - k0).astype(BF16)
    s1 = jnp.dot(diag_inverses[1], panel1, preferred_element_type=F32).astype(BF16)
    return update(me.reshape(1).astype(jnp.int32), a_t, col_panels, s0, s1, owner)


def solution(mesh):
    return jax.shard_map(
        local,
        mesh=mesh,
        in_specs=(P(None, AXES), P(None, AXES, None), P()),
        out_specs=P(AXES, None),
        check_vma=False,
    )
```

```python
import jax
import jax.numpy as jnp
from jax import lax
from jax.experimental import pallas as pl
from jax.experimental.pallas import tpu as pltpu
from jax.sharding import PartitionSpec as P

AXES = ("rows", "rhs")
F32 = jnp.float32
BF16 = jnp.bfloat16
LANES = 128
NT = (((1,), (1,)), ((), ()))
LIMIT = pltpu.CompilerParams(vmem_limit_bytes=58 << 20)
FREE = pl.CostEstimate(flops=0, bytes_accessed=0, transcendentals=0)
ANY = pl.BlockSpec(memory_space=pl.ANY)


def send(x, pairs):
    return lax.ppermute(x, AXES, pairs)


def after(value, *tokens):
    return lax.optimization_barrier((value, *tokens))[0]


def cut(pos, x_t, masks, rows, *tokens):
    width = x_t.shape[0]
    count = len(masks)

    def kernel(pos_ref, *refs):
        for src, dst in zip(refs[:count], refs[-count:]):
            dst[...] = src[...]

    def spec(mask):
        return pl.BlockSpec((width, rows), lambda i, p: (0, p[0] ^ mask))

    whole = pl.BlockSpec((width, rows), lambda i, p: (0, 0))
    return pl.pallas_call(
        kernel,
        out_shape=[jax.ShapeDtypeStruct((width, rows), x_t.dtype)] * count,
        grid_spec=pltpu.PrefetchScalarGridSpec(
            num_scalar_prefetch=1,
            grid=(1,),
            in_specs=[spec(m) for m in masks] + [ANY] * len(tokens),
            out_specs=[whole] * count,
        ),
        compiler_params=LIMIT,
        cost_estimate=FREE,
        name="cut",
    )(pos, *[x_t] * count, *tokens)


def held_rows(tm, pos, i, owner, panel_rows):
    in_panel = i * tm < panel_rows
    return jnp.logical_and(in_panel, jnp.logical_or(pos == 0, pos == owner))


def solve_update(pos, rs0, rs1, block, diag, cols, owner, half, offs0, offs1, offs2):
    rows, nb = cols.shape[1:]
    width = rs0[0].shape[1]
    members = width * len(offs0)
    tm = 256
    wide = BF16 if width % 16 == 0 else F32

    def gather(dst, pair, offs, wrap):
        height = pair[0].shape[1]
        count = pair[0].shape[0]
        for j, off in enumerate(offs):
            ref = pair[j // count]
            at = pl.multiple_of(((wrap ^ off) & (len(offs) - 1)) * height, height)
            dst[pl.ds(at, height), :] = ref[j % count].astype(dst.dtype)

    def dot_nt(a, b):
        return lax.dot_general(a.astype(BF16), b, NT, preferred_element_type=F32)

    def kernel(pos_ref, a0, b0, a1, b1, a2, b2, d_ref, c_ref, o_ref, g0, g1, g2, s0, s1):
        i = pl.program_id(0)
        pos = pos_ref[0]
        upper = pos >= owner
        chunk = 256

        @pl.when(i == 0)
        def _():
            gather(g0, (a0, b0), offs0, pos)

            @pl.loop(0, members // chunk)
            def _(t):
                at = pl.ds(pl.multiple_of(t * chunk, chunk), chunk)
                s0[at, :] = dot_nt(g0[at, :], d_ref[0]).astype(BF16)

            @pl.when(upper)
            def _():
                gather(g1, (a1, b1), offs1, pos)
                gather(g2, (a2, b2), offs2, pos)

                @pl.loop(0, members // chunk)
                def _(t):
                    at = pl.ds(pl.multiple_of(t * chunk, chunk), chunk)
                    panel = g1[at, :].astype(F32) - dot_nt(s0[at, :], g2[...])
                    s1[at, :] = dot_nt(panel, d_ref[1]).astype(BF16)

        held = held_rows(tm, pos, i, owner, nb)
        start = pl.multiple_of(jnp.where(held, i, 0) * tm, tm)

        @pl.when(jnp.logical_not(held))
        def _():
            o_ref[...] = -dot_nt(c_ref[0], s0[...])

            @pl.when(upper)
            def _():
                o_ref[...] -= dot_nt(c_ref[1], s1[...])

        @pl.when(jnp.logical_and(held, pos == 0))
        def _():
            o_ref[...] = s0[:, pl.ds(start, tm)].astype(F32).T

        @pl.when(jnp.logical_and(held, pos == owner))
        def _():
            o_ref[...] = s1[:, pl.ds(start, tm)].astype(F32).T

    def full(x):
        zeros = (0,) * x.ndim
        return pl.BlockSpec(x.shape, lambda i, p: zeros)

    ins = [*rs0, *rs1, *block, diag]
    return pl.pallas_call(
        kernel,
        out_shape=jax.ShapeDtypeStruct((rows, members), F32),
        grid_spec=pltpu.PrefetchScalarGridSpec(
            num_scalar_prefetch=1,
            grid=(rows // tm,),
            in_specs=[full(x) for x in ins] + [pl.BlockSpec((2, tm, nb), lambda i, p: (0, i, 0))],
            out_specs=pl.BlockSpec((tm, members), lambda i, p: (i, 0)),
            scratch_shapes=[
                pltpu.VMEM((members, nb), wide),
                pltpu.VMEM((members, nb), wide),
                pltpu.VMEM((nb, nb), BF16),
                pltpu.VMEM((members, nb), BF16),
                pltpu.VMEM((members, nb), BF16),
            ],
        ),
        compiler_params=LIMIT,
        cost_estimate=FREE,
        name="solve_update",
    )(pos, *ins, cols)


def add_own(pos, v, own, owner, nb, half):
    rows = v.shape[0]
    width = own.shape[1]
    per = LANES // width
    tm = 1024

    def kernel(pos_ref, v_ref, a_ref, o_ref):
        held = held_rows(tm, pos_ref[0], pl.program_id(1), owner, nb)
        turned = a_ref[...].astype(F32).reshape(LANES, tm).T
        o_ref[...] = v_ref[...] + jnp.where(held, 0.0, turned)

    groups = half // per

    def place(j, i, p):
        return (i, jnp.where(p[0] < half, j, j + groups))

    return pl.pallas_call(
        kernel,
        out_shape=jax.ShapeDtypeStruct(v.shape, F32),
        grid_spec=pltpu.PrefetchScalarGridSpec(
            num_scalar_prefetch=1,
            grid=(groups, rows // tm),
            in_specs=[
                pl.BlockSpec((tm, LANES), place),
                pl.BlockSpec((per, width, tm), lambda j, i, p: (j, 0, i)),
            ],
            out_specs=pl.BlockSpec((tm, LANES), place),
        ),
        input_output_aliases={1: 0},
        compiler_params=LIMIT,
        cost_estimate=FREE,
        name="add_own",
    )(pos, v, own)


def add_group(pos, v, parts, masks, owner, nb):
    rows = v.shape[0]
    width = parts[0].shape[0]
    per = len(masks)
    tm = 1024

    def kernel(pos_ref, v_ref, *refs):
        o_ref, turn = refs[per:]
        pos = pos_ref[0]
        held = held_rows(tm, pos, pl.program_id(0), owner, nb)
        for ref, mask in zip(refs[:per], masks):
            at = ((pos ^ mask) & (per - 1)) * width
            turn[pl.ds(pl.multiple_of(at, 8), width), :] = ref[...].astype(F32)
        o_ref[...] = v_ref[...] + jnp.where(held, 0.0, turn[...].T)

    def place(i, p):
        return (i, (p[0] ^ masks[0]) // per)

    return pl.pallas_call(
        kernel,
        out_shape=jax.ShapeDtypeStruct(v.shape, F32),
        grid_spec=pltpu.PrefetchScalarGridSpec(
            num_scalar_prefetch=1,
            grid=(rows // tm,),
            in_specs=[pl.BlockSpec((tm, LANES), place)]
            + [pl.BlockSpec((width, tm), lambda i, p: (0, i))] * per,
            out_specs=pl.BlockSpec((tm, LANES), place),
            scratch_shapes=[pltpu.VMEM((LANES, tm), F32)],
        ),
        input_output_aliases={1: 0},
        compiler_params=LIMIT,
        cost_estimate=FREE,
        name="add_group",
    )(pos, v, *parts)


def local(right_sides, col_panels, diag_inverses):
    n = lax.axis_size("rows") * lax.axis_size("rhs")
    me = lax.axis_index(AXES).astype(jnp.int32)
    pos = me.reshape(1)
    nb = diag_inverses.shape[1]
    total_rows, width = right_sides.shape
    rows = total_rows // n
    half = n // 2
    owner = half
    per = LANES // width
    x_t = right_sides.T

    def every(mask):
        return [(i, i ^ mask) for i in range(n)]

    def upper(mask):
        return [(i, i ^ mask) for i in range(half, n)]

    big = {}

    def launch(masks, *tokens):
        for m, piece in zip(masks, cut(pos, x_t, masks, rows, *tokens)):
            big[m] = send(piece, every(m))
        return [big[m] for m in masks]

    inner = [1 << k for k in range(1, half.bit_length() - 1)][::-1]
    steps = len(inner)
    turn = [inner[t % steps :] + inner[: t % steps] + [1] for t in range(3)]
    todo = list(range(half, n))

    class Chain:
        def __init__(self, cur, offs, pairs, bits):
            self.cur, self.offs, self.pairs, self.bits = cur, offs, pairs, bits
            self.last = []

        def step(self, with_big):
            bit = self.bits.pop(0)
            cur = after(self.cur, *self.last) if self.last else self.cur
            if with_big:
                self.last = launch([todo.pop(0)], *self.last)
            got = send(cur, self.pairs(bit))
            self.offs = self.offs + [o ^ bit for o in self.offs]
            self.pair = (cur, got)
            if self.bits:
                self.cur = jnp.concatenate([cur, got], axis=0)

    own0 = x_t[:, :nb][None]
    own1 = x_t[:, total_rows // 2 : total_rows // 2 + nb][None]
    c0 = Chain(own0, [0], every, [half] + turn[0])
    c1 = Chain(own1, [0], lambda m: upper(m) if m < half else [(i, i + half) for i in range(half)], [half] + turn[1])

    piece = nb // half
    slots = col_panels[0, :nb].reshape(half // 2, 2, piece, nb)
    odd = send(slots[:, 1], [(owner, owner + 1)])
    c0.step(True)
    c1.step(True)
    mine = jnp.where(me == owner, slots[:, 0], odd)
    got = mine[0]
    for t in range(1, half // 2):
        here = send(mine[t], [(owner, owner + 2 * t), (owner + 1, owner + 1 + 2 * t)])
        got = jnp.where(me // 2 == owner // 2 + t, here, got)
    c2 = Chain(got[None], [0], upper, list(turn[2]))
    for step in range(steps + 1):
        c0.step(True)
        c1.step(True)
        c2.step(False)

    ends = [c0.pair[1], c1.pair[1], c2.pair[1]]
    first = jnp.where(after(me, *ends) < half, 0, half * rows)
    own_rows = lax.dynamic_slice_in_dim(right_sides, first, half * rows, 0)
    halves = [list(range(half)), list(range(half, n))]
    own = lax.all_to_all(
        own_rows, AXES, split_axis=0, concat_axis=1, axis_index_groups=halves, tiled=True
    ).T.reshape(half, width, rows)
    tokens = c0.last + c1.last
    while todo:
        now, todo = todo[:3], todo[3:]
        tokens = launch(now, *tokens)

    v = solve_update(
        pos, c0.pair, c1.pair, c2.pair, diag_inverses, col_panels,
        owner, half, c0.offs, c1.offs, c2.offs,
    )
    v = add_own(pos, v, own, owner, nb, half)
    for m in range(half, n, per):
        masks = list(range(m, m + per))
        v = add_group(pos, v, [big[k] for k in masks], masks, owner, nb)
    return v


def solution(mesh):
    return jax.shard_map(
        local,
        mesh=mesh,
        in_specs=(P(None, AXES), P(None, AXES, None), P()),
        out_specs=P(AXES, None),
        check_vma=False,
    )
```

```python
import jax
import jax.numpy as jnp
from jax import lax
from jax.experimental import pallas as pl
from jax.experimental.pallas import tpu as pltpu
from jax.sharding import PartitionSpec as P

AXES = ("rows", "rhs")
F32 = jnp.float32
BF16 = jnp.bfloat16
NT = (((1,), (1,)), ((), ()))
LIMIT = pltpu.CompilerParams(vmem_limit_bytes=58 << 20)
FREE = pl.CostEstimate(flops=0, bytes_accessed=0, transcendentals=0)
ANY = pl.BlockSpec(memory_space=pl.ANY)


def send(x, pairs):
    return lax.ppermute(x, AXES, pairs)


def after(value, *tokens):
    return lax.optimization_barrier((value, *tokens))[0]


def held_rows(tm, pos, i, owner, panel_rows):
    in_panel = i * tm < panel_rows
    return jnp.logical_and(in_panel, jnp.logical_or(pos == 0, pos == owner))


def solve_update(pos, rs0, rs1, block, diag, cols, owner, half, offs0, offs1, offs2):
    rows, nb = cols.shape[1:]
    width = rs0[0].shape[1]
    members = width * len(offs0)
    tm = 512
    wide = BF16 if width % 16 == 0 else F32

    def gather(dst, pair, offs, wrap):
        height = pair[0].shape[1]
        count = pair[0].shape[0]
        for j, off in enumerate(offs):
            ref = pair[j // count]
            at = pl.multiple_of(((wrap ^ off) & (len(offs) - 1)) * height, height)
            dst[pl.ds(at, height), :] = ref[j % count].astype(dst.dtype)

    def dot_nt(a, b):
        return lax.dot_general(a.astype(BF16), b, NT, preferred_element_type=F32)

    def kernel(pos_ref, a0, b0, a1, b1, a2, b2, d_ref, c_ref, o_ref, g0, g1, g2, s0, s1):
        i = pl.program_id(0)
        pos = pos_ref[0]
        upper = pos >= owner
        chunk = min(512, members)

        @pl.when(i == 0)
        def _():
            gather(g0, (a0, b0), offs0, pos)

            @pl.loop(0, members // chunk)
            def _(t):
                at = pl.ds(pl.multiple_of(t * chunk, chunk), chunk)
                s0[at, :] = dot_nt(g0[at, :], d_ref[0]).astype(BF16)

            @pl.when(upper)
            def _():
                gather(g1, (a1, b1), offs1, pos)
                @pl.when(pos & 1 == 0)
                def _():
                    gather(g2, (a2,), offs2, pos >> 1)

                @pl.when(pos & 1 == 1)
                def _():
                    gather(g2, (b2,), offs2, pos >> 1)

                @pl.loop(0, members // chunk)
                def _(t):
                    at = pl.ds(pl.multiple_of(t * chunk, chunk), chunk)
                    panel = g1[at, :].astype(F32) - dot_nt(s0[at, :], g2[...])
                    s1[at, :] = dot_nt(panel, d_ref[1]).astype(BF16)

        held = held_rows(tm, pos, i, owner, nb)
        start = pl.multiple_of(jnp.where(held, i, 0) * tm, tm)

        @pl.when(jnp.logical_not(held))
        def _():
            o_ref[...] = -dot_nt(c_ref[0], s0[...])

            @pl.when(upper)
            def _():
                o_ref[...] -= dot_nt(c_ref[1], s1[...])

        @pl.when(jnp.logical_and(held, pos == 0))
        def _():
            o_ref[...] = s0[:, pl.ds(start, tm)].astype(F32).T

        @pl.when(jnp.logical_and(held, pos == owner))
        def _():
            o_ref[...] = s1[:, pl.ds(start, tm)].astype(F32).T

    def full(x):
        zeros = (0,) * x.ndim
        return pl.BlockSpec(x.shape, lambda i, p: zeros)

    ins = [*rs0, *rs1, *block, diag]
    return pl.pallas_call(
        kernel,
        out_shape=jax.ShapeDtypeStruct((rows, members), F32),
        grid_spec=pltpu.PrefetchScalarGridSpec(
            num_scalar_prefetch=1,
            grid=(rows // tm,),
            in_specs=[full(x) for x in ins] + [pl.BlockSpec((2, tm, nb), lambda i, p: (0, i, 0))],
            out_specs=pl.BlockSpec((tm, members), lambda i, p: (i, 0)),
            scratch_shapes=[
                pltpu.VMEM((members, nb), wide),
                pltpu.VMEM((members, nb), wide),
                pltpu.VMEM((nb, nb), BF16),
                pltpu.VMEM((members, nb), BF16),
                pltpu.VMEM((members, nb), BF16),
            ],
        ),
        compiler_params=LIMIT,
        cost_estimate=pl.CostEstimate(
            flops=14 * members * nb * nb, bytes_accessed=24 << 20, transcendentals=0
        ),
        name="solve_update",
    )(pos, *ins, cols)


def finish(pos, v, a_t, owner, nb):
    rows, members = v.shape
    tm = 256

    def kernel(pos_ref, v_ref, a_ref, o_ref):
        held = held_rows(tm, pos_ref[0], pl.program_id(0), owner, nb)
        row = lax.broadcasted_iota(jnp.int32, (tm, tm), 0)
        col = lax.broadcasted_iota(jnp.int32, (tm, tm), 1)
        keep = jnp.logical_and(row == col, jnp.logical_not(held))
        pick = jnp.where(keep, 1.0, 0.0).astype(BF16)
        turned = lax.dot_general(pick, a_ref[...], NT, preferred_element_type=F32)
        o_ref[...] = v_ref[...] + turned

    return pl.pallas_call(
        kernel,
        out_shape=jax.ShapeDtypeStruct(v.shape, F32),
        grid_spec=pltpu.PrefetchScalarGridSpec(
            num_scalar_prefetch=1,
            grid=(rows // tm,),
            in_specs=[
                pl.BlockSpec((tm, members), lambda i, p: (i, 0)),
                pl.BlockSpec((members, tm), lambda i, p: (0, i)),
            ],
            out_specs=pl.BlockSpec((tm, members), lambda i, p: (i, 0)),
        ),
        input_output_aliases={1: 0},
        compiler_params=LIMIT,
        cost_estimate=pl.CostEstimate(flops=0, bytes_accessed=20 << 20, transcendentals=0),
        name="finish",
    )(pos, v, a_t)


def local(right_sides, col_panels, diag_inverses):
    n = lax.axis_size("rows") * lax.axis_size("rhs")
    me = lax.axis_index(AXES).astype(jnp.int32)
    pos = me.reshape(1)
    nb = diag_inverses.shape[1]
    total_rows, width = right_sides.shape
    rows = total_rows // n
    half = n // 2
    owner = half
    x_t = right_sides.T

    def every(mask):
        return [(i, i ^ mask) for i in range(n)]

    def upper(mask):
        return [(i, i ^ mask) for i in range(half, n)]

    def even(mask):
        return [(i, i ^ mask) for i in range(half, n, 2)]

    quarter = half // 2
    both = jnp.stack([x_t[:, :nb], x_t[:, total_rows // 2 : total_rows // 2 + nb]])
    theirs = send(both, every(half))
    cur = [jnp.stack([both[k], theirs[k]]) for k in range(2)]
    offs = [[0, half], [0, half], [0]]

    chips = quarter // 2
    slots = col_panels[0, :nb].reshape(chips, nb // chips, nb)
    got = slots[0]
    for t in range(1, chips):
        here = send(slots[t], [(owner, owner + 2 * t)])
        got = jnp.where(me // 2 == owner // 2 + t, here, got)
    down = send(got, [(i, i + quarter) for i in range(owner, owner + quarter, 2)])
    cur.append(jnp.where(me >= owner + quarter, down, got)[None])

    new = [send(cur[0], every(quarter)), send(cur[1], upper(quarter))]
    for k in range(2):
        cur[k] = jnp.concatenate([cur[k], new[k]], axis=0)
        offs[k] = offs[k] + [o ^ quarter for o in offs[k]]
    cur = list(lax.optimization_barrier(tuple(cur)))

    inner = [1 << k for k in range(1, quarter.bit_length() - 1)][::-1]
    orders = [inner, inner[::-1], inner]
    pairs = [every, upper, even]
    for k in range(len(inner)):
        bits = [order[k] for order in orders]
        new = [send(cur[t], pairs[t](bits[t])) for t in range(3)]
        new = lax.optimization_barrier(tuple(new))
        if k == 0:
            gate = new
        shifts = [bits[0], bits[1], bits[2] >> 1]
        offs = [offs[t] + [o ^ shifts[t] for o in offs[t]] for t in range(3)]
        cur = [jnp.concatenate([cur[t], new[t]], axis=0) for t in range(3)]
    new = [
        send(cur[0], every(1)),
        send(cur[1], upper(1)),
        send(cur[2], [(i, i + 1) for i in range(half, n, 2)]),
    ]
    ends = [(cur[t], new[t]) for t in range(3)]
    offs = [offs[t] + [o ^ 1 for o in offs[t]] for t in range(2)] + [offs[2]]

    tiles = x_t.reshape(width // 8, 8, n, rows).transpose(2, 0, 1, 3)
    packed = tiles.reshape(n, width, rows)
    a_t = lax.all_to_all(after(packed, *gate), AXES, split_axis=0, concat_axis=0, tiled=True)
    a_t = a_t.reshape(n * width, rows)
    v = solve_update(pos, *ends, diag_inverses, col_panels, owner, half, *offs)
    return finish(pos, v, a_t, owner, nb)


def solution(mesh):
    return jax.shard_map(
        local,
        mesh=mesh,
        in_specs=(P(None, AXES), P(None, AXES, None), P()),
        out_specs=P(AXES, None),
        check_vma=False,
    )
```

```python
import jax
import jax.numpy as jnp
from jax import lax
from jax.experimental import pallas as pl
from jax.experimental.pallas import tpu as pltpu
from jax.sharding import PartitionSpec as P

AXES = ("rows", "rhs")
F32 = jnp.float32
BF16 = jnp.bfloat16
NT = (((1,), (1,)), ((), ()))
FREE = pl.CostEstimate(flops=0, bytes_accessed=0, transcendentals=0)
LIMIT = pltpu.CompilerParams(vmem_limit_bytes=58 << 20)


def send(x, pairs):
    return lax.ppermute(x, AXES, pairs)


def after(value, *tokens):
    return lax.optimization_barrier((value, *tokens))[0]


def collect(dst, refs, offs, where):
    height = refs[0].shape[1]
    count = refs[0].shape[0]
    for j, off in enumerate(offs):
        at = pl.multiple_of(((where ^ off) & (len(offs) - 1)) * height, height)
        dst[pl.ds(at, height), :] = refs[j // count][j % count].astype(dst.dtype)


def dot_nt(a, b):
    return lax.dot_general(a.astype(BF16), b.astype(BF16), NT, preferred_element_type=F32)


def full(x):
    zeros = (0,) * x.ndim
    return pl.BlockSpec(x.shape, lambda i, p: zeros)


def lines_of(width):
    return BF16 if width % 16 == 0 else F32


def first_panel(pos, rs0, diag, cols, owner, offs):
    rows, nb = cols.shape[1:]
    width = rs0[0].shape[1]
    members = width * len(offs)
    tm = 512

    def kernel(pos_ref, a0, b0, d_ref, c_ref, s_ref, o_ref, g0):
        i = pl.program_id(0)
        pos = pos_ref[0]
        chunk = min(512, members)

        @pl.when(i == 0)
        def _():
            collect(g0, (a0, b0), offs, pos)

            @pl.loop(0, members // chunk)
            def _(t):
                at = pl.ds(pl.multiple_of(t * chunk, chunk), chunk)
                s_ref[at, :] = dot_nt(g0[at, :], d_ref[0]).astype(BF16)

        held = jnp.logical_and(pos == 0, i * tm < nb)
        start = pl.multiple_of(jnp.where(held, i, 0) * tm, tm)

        @pl.when(held)
        def _():
            o_ref[...] = s_ref[:, pl.ds(start, tm)].astype(F32).T

        @pl.when(jnp.logical_not(held))
        def _():
            o_ref[...] = -dot_nt(c_ref[0], s_ref[...])

    return pl.pallas_call(
        kernel,
        out_shape=[
            jax.ShapeDtypeStruct((members, nb), BF16),
            jax.ShapeDtypeStruct((rows, members), F32),
        ],
        grid_spec=pltpu.PrefetchScalarGridSpec(
            num_scalar_prefetch=1,
            grid=(rows // tm,),
            in_specs=[
                full(rs0[0]),
                full(rs0[1]),
                pl.BlockSpec((1, nb, nb), lambda i, p: (0, 0, 0)),
                pl.BlockSpec((1, tm, nb), lambda i, p: (0, i, 0)),
            ],
            out_specs=[
                pl.BlockSpec((members, nb), lambda i, p: (0, 0)),
                pl.BlockSpec((tm, members), lambda i, p: (i, 0)),
            ],
            scratch_shapes=[pltpu.VMEM((members, nb), lines_of(width))],
        ),
        compiler_params=LIMIT,
        cost_estimate=FREE,
        name="first_panel",
    )(pos, *rs0, diag, cols)


def second_panel(pos, s0, rs1, block, diag, owner, offs1, offs2):
    members, nb = s0.shape
    width = rs1[0].shape[1]

    def kernel(pos_ref, s0_ref, a1, b1, a2, b2, d_ref, s_ref, g1, g2):
        pos = pos_ref[0]
        chunk = min(512, members)

        @pl.when(pos < owner)
        def _():
            s_ref[...] = jnp.zeros(s_ref.shape, BF16)

        @pl.when(pos >= owner)
        def _():
            collect(g1, (a1, b1), offs1, pos)

            @pl.when(pos & 1 == 0)
            def _():
                collect(g2, (a2,), offs2, pos >> 1)

            @pl.when(pos & 1 == 1)
            def _():
                collect(g2, (b2,), offs2, pos >> 1)

            @pl.loop(0, members // chunk)
            def _(t):
                at = pl.ds(pl.multiple_of(t * chunk, chunk), chunk)
                panel = g1[at, :].astype(F32) - dot_nt(s0_ref[at, :], g2[...])
                s_ref[at, :] = dot_nt(panel, d_ref[0]).astype(BF16)

    ins = [s0, *rs1, *block]
    return pl.pallas_call(
        kernel,
        out_shape=jax.ShapeDtypeStruct((members, nb), BF16),
        grid_spec=pltpu.PrefetchScalarGridSpec(
            num_scalar_prefetch=1,
            grid=(1,),
            in_specs=[full(x) for x in ins] + [pl.BlockSpec((1, nb, nb), lambda i, p: (1, 0, 0))],
            out_specs=pl.BlockSpec((members, nb), lambda i, p: (0, 0)),
            scratch_shapes=[
                pltpu.VMEM((members, nb), lines_of(width)),
                pltpu.VMEM((nb, nb), BF16),
            ],
        ),
        compiler_params=LIMIT,
        cost_estimate=pl.CostEstimate(
            flops=4 * members * nb * nb, bytes_accessed=12 << 20, transcendentals=0
        ),
        name="second_panel",
    )(pos, *ins, diag)


def finish(pos, v, a_t, s1, cols, owner):
    rows, members = v.shape
    nb = s1.shape[1]
    tm = 512

    def kernel(pos_ref, v_ref, a_ref, s_ref, c_ref, o_ref):
        i = pl.program_id(0)
        pos = pos_ref[0]
        panel = i * tm < nb
        kept = jnp.logical_and(pos == 0, panel)
        solved = jnp.logical_and(pos == owner, panel)

        @pl.when(kept)
        def _():
            o_ref[...] = v_ref[...]

        @pl.when(solved)
        def _():
            start = pl.multiple_of(jnp.where(solved, i, 0) * tm, tm)
            o_ref[...] = s_ref[:, pl.ds(start, tm)].astype(F32).T

        @pl.when(jnp.logical_not(jnp.logical_or(kept, solved)))
        def _():
            base = v_ref[...] + a_ref[...].T.astype(F32)

            @pl.when(pos < owner)
            def _():
                o_ref[...] = base

            @pl.when(pos >= owner)
            def _():
                o_ref[...] = base - dot_nt(c_ref[0], s_ref[...])

    def part(i, p):
        return (1, jnp.where(p[0] < owner, 0, i), 0)

    return pl.pallas_call(
        kernel,
        out_shape=jax.ShapeDtypeStruct(v.shape, F32),
        grid_spec=pltpu.PrefetchScalarGridSpec(
            num_scalar_prefetch=1,
            grid=(rows // tm,),
            in_specs=[
                pl.BlockSpec((tm, members), lambda i, p: (i, 0)),
                pl.BlockSpec((members, tm), lambda i, p: (0, i)),
                full(s1),
                pl.BlockSpec((1, tm, nb), part),
            ],
            out_specs=pl.BlockSpec((tm, members), lambda i, p: (i, 0)),
        ),
        compiler_params=LIMIT,
        cost_estimate=pl.CostEstimate(
            flops=2 * rows * members * nb, bytes_accessed=26 << 20, transcendentals=0
        ),
        name="finish",
    )(pos, v, a_t, s1, cols)


def local(right_sides, col_panels, diag_inverses):
    n = lax.axis_size("rows") * lax.axis_size("rhs")
    me = lax.axis_index(AXES).astype(jnp.int32)
    pos = me.reshape(1)
    nb = diag_inverses.shape[1]
    total_rows, width = right_sides.shape
    rows = total_rows // n
    half = n // 2
    owner = half
    x_t = right_sides.T

    def every(mask):
        return [(i, i ^ mask) for i in range(n)]

    def upper(mask):
        return [(i, i ^ mask) for i in range(half, n)]

    def even(mask):
        return [(i, i ^ mask) for i in range(half, n, 2)]

    quarter = half // 2
    both = jnp.stack([x_t[:, :nb], x_t[:, total_rows // 2 : total_rows // 2 + nb]])
    theirs = send(both, every(half))
    cur = [jnp.stack([both[k], theirs[k]]) for k in range(2)]
    offs = [[0, half], [0, half], [0]]

    chips = quarter // 2
    slots = after(col_panels[0, :nb], both).reshape(chips, nb // chips, nb)
    got = slots[0]
    for t in range(1, chips):
        here = send(slots[t], [(owner, owner + 2 * t)])
        got = jnp.where(me // 2 == owner // 2 + t, here, got)
    down = send(got, [(i, i + quarter) for i in range(owner, owner + quarter, 2)])
    cur.append(jnp.where(me >= owner + quarter, down, got)[None])

    new = (send(cur[0], every(quarter)), send(cur[1], upper(quarter)))
    new = lax.optimization_barrier(new)
    for k in range(2):
        cur[k] = jnp.concatenate([cur[k], new[k]], axis=0)
        offs[k] = offs[k] + [o ^ quarter for o in offs[k]]

    inner = [1 << k for k in range(1, quarter.bit_length() - 1)][::-1]
    orders = [inner, inner[::-1], inner]

    def phase(t, k, pairs):
        bit = orders[t][k]
        got = send(cur[t], pairs(bit))
        offs[t] = offs[t] + [o ^ (bit >> 1 if t == 2 else bit) for o in offs[t]]
        return got

    def grow(new):
        for t, got in enumerate(new):
            cur[t] = jnp.concatenate([cur[t], got], axis=0)

    new = lax.optimization_barrier((phase(0, 0, every), phase(1, 0, upper)))
    gate = [*new, cur[2]]
    grow(new)
    for k in range(1, len(inner)):
        new = (phase(0, k, every), phase(1, k, upper), phase(2, k - 1, even))
        new = lax.optimization_barrier(new)
        grow(new)
    rs0 = (cur[0], send(cur[0], every(1)))
    offs = [offs[t] + [o ^ 1 for o in offs[t]] for t in range(2)] + offs[2:]
    got = phase(2, len(inner) - 1, even)
    s0, v = first_panel(pos, rs0, diag_inverses, col_panels, owner, offs[0])
    rs1 = (cur[1], send(cur[1], upper(1)))
    last = jnp.concatenate([cur[2], after(got, s0)], axis=0)
    block = (last, send(last, [(i, i + 1) for i in range(half, n, 2)]))

    tiles = x_t.reshape(width // 8, 8, n, rows).transpose(2, 0, 1, 3)
    packed = tiles.reshape(n, width, rows)
    a_t = lax.all_to_all(after(packed, *gate), AXES, split_axis=0, concat_axis=0, tiled=True)
    a_t = a_t.reshape(n * width, rows)
    s1 = second_panel(pos, s0, rs1, block, diag_inverses, owner, offs[1], offs[2])
    return finish(pos, v, a_t, s1, col_panels, owner)


def solution(mesh):
    return jax.shard_map(
        local,
        mesh=mesh,
        in_specs=(P(None, AXES), P(None, AXES, None), P()),
        out_specs=P(AXES, None),
        check_vma=False,
    )
```

```python
import jax
import jax.numpy as jnp
from jax import lax
from jax.experimental import pallas as pl
from jax.experimental.pallas import tpu as pltpu
from jax.sharding import PartitionSpec as P

AXES = ("rows", "rhs")
F32 = jnp.float32
BF16 = jnp.bfloat16
NT = (((1,), (1,)), ((), ()))
LIMIT = pltpu.CompilerParams(vmem_limit_bytes=58 << 20)
FREE = pl.CostEstimate(flops=0, bytes_accessed=0, transcendentals=0)
ANY = pl.BlockSpec(memory_space=pl.ANY)


def send(x, pairs):
    return lax.ppermute(x, AXES, pairs)


def after(value, *tokens):
    return lax.optimization_barrier((value, *tokens))[0]


def held_rows(tm, pos, i, owner, panel_rows):
    in_panel = i * tm < panel_rows
    return jnp.logical_and(in_panel, jnp.logical_or(pos == 0, pos == owner))


def solve_update(pos, rs0, rs1, block, diag, cols, owner, half, offs0, offs1, offs2):
    rows, nb = cols.shape[1:]
    width = rs0[0].shape[1]
    members = width * len(offs0)
    tm = 512
    wide = BF16 if width % 16 == 0 else F32

    def gather(dst, pair, offs, wrap):
        height = pair[0].shape[1]
        count = pair[0].shape[0]
        for j, off in enumerate(offs):
            ref = pair[j // count]
            at = pl.multiple_of(((wrap ^ off) & (len(offs) - 1)) * height, height)
            dst[pl.ds(at, height), :] = ref[j % count].astype(dst.dtype)

    def dot_nt(a, b):
        return lax.dot_general(a.astype(BF16), b, NT, preferred_element_type=F32)

    def kernel(pos_ref, a0, b0, a1, b1, a2, b2, d_ref, c_ref, o_ref, g0, g1, g2, s0, s1):
        i = pl.program_id(0)
        pos = pos_ref[0]
        upper = pos >= owner
        chunk = min(512, members)

        @pl.when(i == 0)
        def _():
            gather(g0, (a0, b0), offs0, pos)

            @pl.loop(0, members // chunk)
            def _(t):
                at = pl.ds(pl.multiple_of(t * chunk, chunk), chunk)
                s0[at, :] = dot_nt(g0[at, :], d_ref[0]).astype(BF16)

            @pl.when(upper)
            def _():
                gather(g1, (a1, b1), offs1, pos)
                @pl.when(pos & 1 == 0)
                def _():
                    gather(g2, (a2,), offs2, pos >> 1)

                @pl.when(pos & 1 == 1)
                def _():
                    gather(g2, (b2,), offs2, pos >> 1)

                @pl.loop(0, members // chunk)
                def _(t):
                    at = pl.ds(pl.multiple_of(t * chunk, chunk), chunk)
                    panel = g1[at, :].astype(F32) - dot_nt(s0[at, :], g2[...])
                    s1[at, :] = dot_nt(panel, d_ref[1]).astype(BF16)

        held = held_rows(tm, pos, i, owner, nb)
        start = pl.multiple_of(jnp.where(held, i, 0) * tm, tm)

        @pl.when(jnp.logical_not(held))
        def _():
            o_ref[...] = -dot_nt(c_ref[0], s0[...])

            @pl.when(upper)
            def _():
                o_ref[...] -= dot_nt(c_ref[1], s1[...])

        @pl.when(jnp.logical_and(held, pos == 0))
        def _():
            o_ref[...] = s0[:, pl.ds(start, tm)].astype(F32).T

        @pl.when(jnp.logical_and(held, pos == owner))
        def _():
            o_ref[...] = s1[:, pl.ds(start, tm)].astype(F32).T

    def full(x):
        zeros = (0,) * x.ndim
        return pl.BlockSpec(x.shape, lambda i, p: zeros)

    ins = [*rs0, *rs1, *block, diag]
    return pl.pallas_call(
        kernel,
        out_shape=jax.ShapeDtypeStruct((rows, members), F32),
        grid_spec=pltpu.PrefetchScalarGridSpec(
            num_scalar_prefetch=1,
            grid=(rows // tm,),
            in_specs=[full(x) for x in ins] + [pl.BlockSpec((2, tm, nb), lambda i, p: (0, i, 0))],
            out_specs=pl.BlockSpec((tm, members), lambda i, p: (i, 0)),
            scratch_shapes=[
                pltpu.VMEM((members, nb), wide),
                pltpu.VMEM((members, nb), wide),
                pltpu.VMEM((nb, nb), BF16),
                pltpu.VMEM((members, nb), BF16),
                pltpu.VMEM((members, nb), BF16),
            ],
        ),
        compiler_params=LIMIT,
        cost_estimate=pl.CostEstimate(
            flops=14 * members * nb * nb, bytes_accessed=24 << 20, transcendentals=0
        ),
        name="solve_update",
    )(pos, *ins, cols)


def finish(pos, v, a_t, owner, nb):
    rows, members = v.shape
    tm = 512

    def kernel(pos_ref, v_ref, a_ref, o_ref):
        held = held_rows(tm, pos_ref[0], pl.program_id(0), owner, nb)
        o_ref[...] = v_ref[...] + jnp.where(held, 0.0, a_ref[...].T.astype(F32))

    return pl.pallas_call(
        kernel,
        out_shape=jax.ShapeDtypeStruct(v.shape, F32),
        grid_spec=pltpu.PrefetchScalarGridSpec(
            num_scalar_prefetch=1,
            grid=(rows // tm,),
            in_specs=[
                pl.BlockSpec((tm, members), lambda i, p: (i, 0)),
                pl.BlockSpec((members, tm), lambda i, p: (0, i)),
            ],
            out_specs=pl.BlockSpec((tm, members), lambda i, p: (i, 0)),
        ),
        input_output_aliases={1: 0},
        compiler_params=LIMIT,
        cost_estimate=pl.CostEstimate(flops=0, bytes_accessed=20 << 20, transcendentals=0),
        name="finish",
    )(pos, v, a_t)


def local(right_sides, col_panels, diag_inverses):
    n = lax.axis_size("rows") * lax.axis_size("rhs")
    me = lax.axis_index(AXES).astype(jnp.int32)
    pos = me.reshape(1)
    nb = diag_inverses.shape[1]
    total_rows, width = right_sides.shape
    rows = total_rows // n
    half = n // 2
    owner = half
    x_t = right_sides.T

    def every(mask):
        return [(i, i ^ mask) for i in range(n)]

    def upper(mask):
        return [(i, i ^ mask) for i in range(half, n)]

    def even(mask):
        return [(i, i ^ mask) for i in range(half, n, 2)]

    quarter = half // 2
    both = jnp.stack([x_t[:, :nb], x_t[:, total_rows // 2 : total_rows // 2 + nb]])
    theirs = send(both, every(half))
    cur = [jnp.stack([both[k], theirs[k]]) for k in range(2)]
    offs = [[0, half], [0, half], [0]]

    chips = quarter // 2
    slots = after(col_panels[0, :nb], both).reshape(chips, nb // chips, nb)
    got = slots[0]
    for t in range(1, chips):
        here = send(slots[t], [(owner, owner + 2 * t)])
        got = jnp.where(me // 2 == owner // 2 + t, here, got)
    down = send(got, [(i, i + quarter) for i in range(owner, owner + quarter, 2)])
    cur.append(jnp.where(me >= owner + quarter, down, got)[None])

    new = (send(cur[0], every(quarter)), send(cur[1], upper(quarter)))
    new = lax.optimization_barrier(new)
    for k in range(2):
        cur[k] = jnp.concatenate([cur[k], new[k]], axis=0)
        offs[k] = offs[k] + [o ^ quarter for o in offs[k]]

    inner = [1 << k for k in range(1, quarter.bit_length() - 1)][::-1]
    orders = [inner, inner[::-1]]
    pairs = [every, upper]

    def phase(t, k):
        bit = orders[t][k]
        offs[t] = offs[t] + [o ^ bit for o in offs[t]]
        return send(cur[t], pairs[t](bit))

    def grow(new):
        for t, got in enumerate(new):
            cur[t] = jnp.concatenate([cur[t], *got], axis=0)

    last = len(inner) - 1
    for k in range(last):
        new = [[phase(0, k)], [phase(1, k)]]
        if k < last - 1:
            new.append([send(cur[2], even(inner[k]))])
            offs[2] = offs[2] + [o ^ (inner[k] >> 1) for o in offs[2]]
        new = lax.optimization_barrier(new)
        if k == 0:
            gate = [*new, cur[2]]
        grow(new)
    ends = [inner[-1] ^ inner[-2], inner[-1], inner[-2]]
    new = [[phase(0, last)], [phase(1, last)], [send(cur[2], even(m)) for m in ends]]
    offs[2] = offs[2] + [o ^ (m >> 1) for m in ends for o in offs[2]]
    grow(lax.optimization_barrier(new))
    rs0 = (cur[0], send(cur[0], every(1)))
    rs1 = (cur[1], send(cur[1], upper(1)))
    block = (cur[2], send(cur[2], [(i, i + 1) for i in range(half, n, 2)]))
    offs = [offs[t] + [o ^ 1 for o in offs[t]] for t in range(2)] + offs[2:]

    tiles = x_t.reshape(width // 8, 8, n, rows).transpose(2, 0, 1, 3)
    packed = tiles.reshape(n, width, rows)
    a_t = lax.all_to_all(after(packed, gate), AXES, split_axis=0, concat_axis=0, tiled=True)
    a_t = a_t.reshape(n * width, rows)
    v = solve_update(
        pos, rs0, rs1, block, diag_inverses, col_panels, owner, half, *offs
    )
    return finish(pos, v, a_t, owner, nb)


def solution(mesh):
    return jax.shard_map(
        local,
        mesh=mesh,
        in_specs=(P(None, AXES), P(None, AXES, None), P()),
        out_specs=P(AXES, None),
        check_vma=False,
    )
```

```python
import jax
import jax.numpy as jnp
from jax import lax
from jax.experimental import pallas as pl
from jax.experimental.pallas import tpu as pltpu
from jax.sharding import PartitionSpec as P

AXES = ("rows", "rhs")
F32 = jnp.float32
BF16 = jnp.bfloat16
NT = (((1,), (1,)), ((), ()))
LIMIT = pltpu.CompilerParams(vmem_limit_bytes=34 << 20)
FREE = pl.CostEstimate(flops=0, bytes_accessed=0, transcendentals=0)
ANY = pl.BlockSpec(memory_space=pl.ANY)


def send(x, pairs):
    return lax.ppermute(x, AXES, pairs)


def after(value, *tokens):
    return lax.optimization_barrier((value, *tokens))[0]


def held_rows(tm, pos, i, owner, panel_rows):
    in_panel = i * tm < panel_rows
    return jnp.logical_and(in_panel, jnp.logical_or(pos == 0, pos == owner))


def solve_update(pos, rs0, rs1, block, diag, cols, owner, half, offs0, offs1, offs2):
    rows, nb = cols.shape[1:]
    width = rs0[0].shape[1]
    members = width * len(offs0)
    tm = 512
    wide = BF16 if width % 16 == 0 else F32

    def gather(dst, pair, offs, wrap):
        height = pair[0].shape[1]
        count = pair[0].shape[0]
        for j, off in enumerate(offs):
            ref = pair[j // count]
            at = pl.multiple_of(((wrap ^ off) & (len(offs) - 1)) * height, height)
            dst[pl.ds(at, height), :] = ref[j % count].astype(dst.dtype)

    def dot_nt(a, b):
        return lax.dot_general(a.astype(BF16), b, NT, preferred_element_type=F32)

    def kernel(pos_ref, a0, b0, a1, b1, a2, b2, d_ref, c_ref, o_ref, g0, g1, g2, s0, s1):
        i = pl.program_id(0)
        pos = pos_ref[0]
        upper = pos >= owner
        chunk = min(512, members)

        @pl.when(i == 0)
        def _():
            gather(g0, (a0, b0), offs0, pos)

            @pl.loop(0, members // chunk)
            def _(t):
                at = pl.ds(pl.multiple_of(t * chunk, chunk), chunk)
                s0[at, :] = dot_nt(g0[at, :], d_ref[0]).astype(BF16)

            @pl.when(upper)
            def _():
                gather(g1, (a1, b1), offs1, pos)
                @pl.when(pos & 1 == 0)
                def _():
                    gather(g2, (a2,), offs2, pos >> 1)

                @pl.when(pos & 1 == 1)
                def _():
                    gather(g2, (b2,), offs2, pos >> 1)

                @pl.loop(0, members // chunk)
                def _(t):
                    at = pl.ds(pl.multiple_of(t * chunk, chunk), chunk)
                    panel = g1[at, :].astype(F32) - dot_nt(s0[at, :], g2[...])
                    s1[at, :] = dot_nt(panel, d_ref[1]).astype(BF16)

        held = held_rows(tm, pos, i, owner, nb)
        start = pl.multiple_of(jnp.where(held, i, 0) * tm, tm)

        @pl.when(jnp.logical_not(held))
        def _():
            o_ref[...] = -dot_nt(c_ref[0], s0[...])

            @pl.when(upper)
            def _():
                o_ref[...] -= dot_nt(c_ref[1], s1[...])

        @pl.when(jnp.logical_and(held, pos == 0))
        def _():
            o_ref[...] = s0[:, pl.ds(start, tm)].astype(F32).T

        @pl.when(jnp.logical_and(held, pos == owner))
        def _():
            o_ref[...] = s1[:, pl.ds(start, tm)].astype(F32).T

    def full(x):
        zeros = (0,) * x.ndim
        return pl.BlockSpec(x.shape, lambda i, p: zeros)

    ins = [*rs0, *rs1, *block, diag]
    return pl.pallas_call(
        kernel,
        out_shape=jax.ShapeDtypeStruct((rows, members), F32),
        grid_spec=pltpu.PrefetchScalarGridSpec(
            num_scalar_prefetch=1,
            grid=(rows // tm,),
            in_specs=[full(x) for x in ins] + [pl.BlockSpec((2, tm, nb), lambda i, p: (0, i, 0))],
            out_specs=pl.BlockSpec((tm, members), lambda i, p: (i, 0)),
            scratch_shapes=[
                pltpu.VMEM((members, nb), wide),
                pltpu.VMEM((members, nb), wide),
                pltpu.VMEM((nb, nb), BF16),
                pltpu.VMEM((members, nb), BF16),
                pltpu.VMEM((members, nb), BF16),
            ],
        ),
        compiler_params=LIMIT,
        cost_estimate=pl.CostEstimate(
            flops=14 * members * nb * nb, bytes_accessed=24 << 20, transcendentals=0
        ),
        name="solve_update",
    )(pos, *ins, cols)


def finish(pos, v, a_t, owner, nb):
    rows, members = v.shape
    tm = 512

    def kernel(pos_ref, v_ref, a_ref, o_ref):
        held = held_rows(tm, pos_ref[0], pl.program_id(0), owner, nb)
        o_ref[...] = v_ref[...] + jnp.where(held, 0.0, a_ref[...].T.astype(F32))

    return pl.pallas_call(
        kernel,
        out_shape=jax.ShapeDtypeStruct(v.shape, F32),
        grid_spec=pltpu.PrefetchScalarGridSpec(
            num_scalar_prefetch=1,
            grid=(rows // tm,),
            in_specs=[
                pl.BlockSpec((tm, members), lambda i, p: (i, 0)),
                pl.BlockSpec((members, tm), lambda i, p: (0, i)),
            ],
            out_specs=pl.BlockSpec((tm, members), lambda i, p: (i, 0)),
        ),
        input_output_aliases={1: 0},
        compiler_params=LIMIT,
        cost_estimate=pl.CostEstimate(flops=0, bytes_accessed=20 << 20, transcendentals=0),
        name="finish",
    )(pos, v, a_t)


def local(right_sides, col_panels, diag_inverses):
    n = lax.axis_size("rows") * lax.axis_size("rhs")
    me = lax.axis_index(AXES).astype(jnp.int32)
    pos = me.reshape(1)
    nb = diag_inverses.shape[1]
    total_rows, width = right_sides.shape
    rows = total_rows // n
    half = n // 2
    owner = half
    x_t = right_sides.T

    def every(mask):
        return [(i, i ^ mask) for i in range(n)]

    def upper(mask):
        return [(i, i ^ mask) for i in range(half, n)]

    def even(mask):
        return [(i, i ^ mask) for i in range(half, n, 2)]

    quarter = half // 2
    both = jnp.stack([x_t[:, :nb], x_t[:, total_rows // 2 : total_rows // 2 + nb]])
    theirs = send(both, every(half))
    cur = [jnp.stack([both[k], theirs[k]]) for k in range(2)]
    offs = [[0, half], [0, half], [0]]

    chips = quarter // 2
    slots = after(col_panels[0, :nb], both).reshape(chips, nb // chips, nb)
    got = slots[0]
    for t in range(1, chips):
        here = send(slots[t], [(owner, owner + 2 * t)])
        got = jnp.where(me // 2 == owner // 2 + t, here, got)
    down = send(got, [(i, i + quarter) for i in range(owner, owner + quarter, 2)])
    cur.append(jnp.where(me >= owner + quarter, down, got)[None])

    new = (send(cur[0], every(quarter)), send(cur[1], upper(quarter)))
    new = lax.optimization_barrier(new)
    for k in range(2):
        cur[k] = jnp.concatenate([cur[k], new[k]], axis=0)
        offs[k] = offs[k] + [o ^ quarter for o in offs[k]]

    inner = [1 << k for k in range(1, quarter.bit_length() - 1)][::-1]
    orders = [inner, inner[::-1]]
    pairs = [every, upper]

    def phase(t, k):
        bit = orders[t][k]
        offs[t] = offs[t] + [o ^ bit for o in offs[t]]
        return send(cur[t], pairs[t](bit))

    def grow(new):
        for t, got in enumerate(new):
            cur[t] = jnp.concatenate([cur[t], *got], axis=0)

    last = len(inner) - 1
    for k in range(last):
        new = [[phase(0, k)], [phase(1, k)]]
        if k < last - 1:
            new.append([send(cur[2], even(inner[k]))])
            offs[2] = offs[2] + [o ^ (inner[k] >> 1) for o in offs[2]]
        new = lax.optimization_barrier(new)
        if k == 0:
            gate = [*new, cur[2]]
        grow(new)
    ends = [inner[-1] ^ inner[-2], inner[-1], inner[-2]]
    new = [[phase(0, last)], [phase(1, last)], [send(cur[2], even(m)) for m in ends]]
    offs[2] = offs[2] + [o ^ (m >> 1) for m in ends for o in offs[2]]
    grow(lax.optimization_barrier(new))
    rs0 = (cur[0], send(cur[0], every(1)))
    rs1 = (cur[1], send(cur[1], upper(1)))
    block = (cur[2], send(cur[2], [(i, i + 1) for i in range(half, n, 2)]))
    offs = [offs[t] + [o ^ 1 for o in offs[t]] for t in range(2)] + offs[2:]

    tiles = x_t.reshape(width // 8, 8, n, rows).transpose(2, 0, 1, 3)
    packed = tiles.reshape(n, width, rows)
    a_t = lax.all_to_all(after(packed, gate), AXES, split_axis=0, concat_axis=0, tiled=True)
    a_t = a_t.reshape(n * width, rows)
    v = solve_update(
        pos, rs0, rs1, block, diag_inverses, col_panels, owner, half, *offs
    )
    return finish(pos, v, a_t, owner, nb)


def solution(mesh):
    return jax.shard_map(
        local,
        mesh=mesh,
        in_specs=(P(None, AXES), P(None, AXES, None), P()),
        out_specs=P(AXES, None),
        check_vma=False,
    )
```

```python
import jax
import jax.numpy as jnp
from jax import lax
from jax.experimental import pallas as pl
from jax.experimental.pallas import tpu as pltpu
from jax.sharding import PartitionSpec as P

AXES = ("rows", "rhs")
F32 = jnp.float32
BF16 = jnp.bfloat16
NT = (((1,), (1,)), ((), ()))
LIMIT = pltpu.CompilerParams(vmem_limit_bytes=34 << 20)
FREE = pl.CostEstimate(flops=0, bytes_accessed=0, transcendentals=0)
ANY = pl.BlockSpec(memory_space=pl.ANY)


def send(x, pairs):
    return lax.ppermute(x, AXES, pairs)


def after(value, *tokens):
    return lax.optimization_barrier((value, *tokens))[0]


def held_rows(tm, pos, i, owner, panel_rows):
    in_panel = i * tm < panel_rows
    return jnp.logical_and(in_panel, jnp.logical_or(pos == 0, pos == owner))


def solve_update(pos, rs0, rs1, block, diag, cols, owner, half, offs0, offs1, offs2):
    rows, nb = cols.shape[1:]
    width = rs0[0].shape[1]
    members = width * len(offs0)
    tm = 512
    wide = BF16 if width % 16 == 0 else F32

    def gather(dst, pair, offs, wrap):
        height = pair[0].shape[1]
        count = pair[0].shape[0]
        for j, off in enumerate(offs):
            ref = pair[j // count]
            at = pl.multiple_of(((wrap ^ off) & (len(offs) - 1)) * height, height)
            dst[pl.ds(at, height), :] = ref[j % count].astype(dst.dtype)

    def dot_nt(a, b):
        return lax.dot_general(a.astype(BF16), b, NT, preferred_element_type=F32)

    def kernel(pos_ref, a0, b0, a1, b1, a2, b2, d_ref, c_ref, o_ref, g0, g1, g2, s0, s1):
        i = pl.program_id(0)
        pos = pos_ref[0]
        upper = pos >= owner
        chunk = min(512, members)

        @pl.when(i == 0)
        def _():
            gather(g0, (a0, b0), offs0, pos)

            @pl.loop(0, members // chunk)
            def _(t):
                at = pl.ds(pl.multiple_of(t * chunk, chunk), chunk)
                s0[at, :] = dot_nt(g0[at, :], d_ref[0]).astype(BF16)

            @pl.when(upper)
            def _():
                gather(g1, (a1, b1), offs1, pos)
                @pl.when(pos & 1 == 0)
                def _():
                    gather(g2, (a2,), offs2, pos >> 1)

                @pl.when(pos & 1 == 1)
                def _():
                    gather(g2, (b2,), offs2, pos >> 1)

                @pl.loop(0, members // chunk)
                def _(t):
                    at = pl.ds(pl.multiple_of(t * chunk, chunk), chunk)
                    panel = g1[at, :].astype(F32) - dot_nt(s0[at, :], g2[...])
                    s1[at, :] = dot_nt(panel, d_ref[1]).astype(BF16)

        held = held_rows(tm, pos, i, owner, nb)
        start = pl.multiple_of(jnp.where(held, i, 0) * tm, tm)

        @pl.when(jnp.logical_not(held))
        def _():
            o_ref[...] = -dot_nt(c_ref[0], s0[...])

            @pl.when(upper)
            def _():
                o_ref[...] -= dot_nt(c_ref[1], s1[...])

        @pl.when(jnp.logical_and(held, pos == 0))
        def _():
            o_ref[...] = s0[:, pl.ds(start, tm)].astype(F32).T

        @pl.when(jnp.logical_and(held, pos == owner))
        def _():
            o_ref[...] = s1[:, pl.ds(start, tm)].astype(F32).T

    def full(x):
        zeros = (0,) * x.ndim
        return pl.BlockSpec(x.shape, lambda i, p: zeros)

    ins = [*rs0, *rs1, *block, diag]
    return pl.pallas_call(
        kernel,
        out_shape=jax.ShapeDtypeStruct((rows, members), F32),
        grid_spec=pltpu.PrefetchScalarGridSpec(
            num_scalar_prefetch=1,
            grid=(rows // tm,),
            in_specs=[full(x) for x in ins] + [pl.BlockSpec((2, tm, nb), lambda i, p: (0, i, 0))],
            out_specs=pl.BlockSpec((tm, members), lambda i, p: (i, 0)),
            scratch_shapes=[
                pltpu.VMEM((members, nb), wide),
                pltpu.VMEM((members, nb), wide),
                pltpu.VMEM((nb, nb), BF16),
                pltpu.VMEM((members, nb), BF16),
                pltpu.VMEM((members, nb), BF16),
            ],
        ),
        compiler_params=LIMIT,
        cost_estimate=pl.CostEstimate(
            flops=14 * members * nb * nb, bytes_accessed=24 << 20, transcendentals=0
        ),
        name="solve_update",
    )(pos, *ins, cols)


def finish(pos, v, a_t, owner, nb):
    rows, members = v.shape
    tm = 512

    def kernel(pos_ref, v_ref, a_ref, o_ref):
        held = held_rows(tm, pos_ref[0], pl.program_id(0), owner, nb)
        o_ref[...] = v_ref[...] + jnp.where(held, 0.0, a_ref[...].T.astype(F32))

    return pl.pallas_call(
        kernel,
        out_shape=jax.ShapeDtypeStruct(v.shape, F32),
        grid_spec=pltpu.PrefetchScalarGridSpec(
            num_scalar_prefetch=1,
            grid=(rows // tm,),
            in_specs=[
                pl.BlockSpec((tm, members), lambda i, p: (i, 0)),
                pl.BlockSpec((members, tm), lambda i, p: (0, i)),
            ],
            out_specs=pl.BlockSpec((tm, members), lambda i, p: (i, 0)),
        ),
        input_output_aliases={1: 0},
        compiler_params=LIMIT,
        cost_estimate=pl.CostEstimate(flops=0, bytes_accessed=20 << 20, transcendentals=0),
        name="finish",
    )(pos, v, a_t)


def local(right_sides, col_panels, diag_inverses):
    n = lax.axis_size("rows") * lax.axis_size("rhs")
    me = lax.axis_index(AXES).astype(jnp.int32)
    pos = me.reshape(1)
    nb = diag_inverses.shape[1]
    total_rows, width = right_sides.shape
    rows = total_rows // n
    half = n // 2
    owner = half
    x_t = right_sides.T

    def every(mask):
        return [(i, i ^ mask) for i in range(n)]

    def upper(mask):
        return [(i, i ^ mask) for i in range(half, n)]

    def even(mask):
        return [(i, i ^ mask) for i in range(half, n, 2)]

    quarter = half // 2
    both = jnp.stack([x_t[:, :nb], x_t[:, total_rows // 2 : total_rows // 2 + nb]])
    theirs = send(both, every(half))
    cur = [jnp.stack([both[k], theirs[k]]) for k in range(2)]
    offs = [[0, half], [0, half], [0]]

    chips = quarter // 2
    piece = nb // chips
    zero = after(jnp.int32(0), both)

    def slot(t):
        return lax.dynamic_slice(col_panels, (zero, t * piece, 0), (1, piece, nb))[0]

    got = slot(0)
    for t in range(1, chips):
        here = send(slot(t), [(owner, owner + 2 * t)])
        got = jnp.where(me // 2 == owner // 2 + t, here, got)
    down = send(got, [(i, i + quarter) for i in range(owner, owner + quarter, 2)])
    cur.append(jnp.where(me >= owner + quarter, down, got)[None])

    new = (send(cur[0], every(quarter)), send(cur[1], upper(quarter)))
    new = lax.optimization_barrier(new)
    for k in range(2):
        cur[k] = jnp.concatenate([cur[k], new[k]], axis=0)
        offs[k] = offs[k] + [o ^ quarter for o in offs[k]]

    inner = [1 << k for k in range(1, quarter.bit_length() - 1)][::-1]
    orders = [inner, inner[::-1]]
    pairs = [every, upper]

    def phase(t, k):
        bit = orders[t][k]
        offs[t] = offs[t] + [o ^ bit for o in offs[t]]
        return send(cur[t], pairs[t](bit))

    def grow(new):
        for t, got in enumerate(new):
            cur[t] = jnp.concatenate([cur[t], *got], axis=0)

    last = len(inner) - 1
    for k in range(last):
        new = [[phase(0, k)], [phase(1, k)]]
        if k < last - 1:
            new.append([send(cur[2], even(inner[k]))])
            offs[2] = offs[2] + [o ^ (inner[k] >> 1) for o in offs[2]]
        new = lax.optimization_barrier(new)
        if k == 0:
            gate = [*new, cur[2]]
        grow(new)
    ends = [inner[-1] ^ inner[-2], inner[-1], inner[-2]]
    new = [[phase(0, last)], [phase(1, last)], [send(cur[2], even(m)) for m in ends]]
    offs[2] = offs[2] + [o ^ (m >> 1) for m in ends for o in offs[2]]
    grow(lax.optimization_barrier(new))
    rs0 = (cur[0], send(cur[0], every(1)))
    rs1 = (cur[1], send(cur[1], upper(1)))
    block = (cur[2], send(cur[2], [(i, i + 1) for i in range(half, n, 2)]))
    offs = [offs[t] + [o ^ 1 for o in offs[t]] for t in range(2)] + offs[2:]

    tiles = x_t.reshape(width // 8, 8, n, rows).transpose(2, 0, 1, 3)
    packed = tiles.reshape(n, width, rows)
    a_t = lax.all_to_all(after(packed, gate), AXES, split_axis=0, concat_axis=0, tiled=True)
    a_t = a_t.reshape(n * width, rows)
    v = solve_update(
        pos, rs0, rs1, block, diag_inverses, col_panels, owner, half, *offs
    )
    return finish(pos, v, a_t, owner, nb)


def solution(mesh):
    return jax.shard_map(
        local,
        mesh=mesh,
        in_specs=(P(None, AXES), P(None, AXES, None), P()),
        out_specs=P(AXES, None),
        check_vma=False,
    )
```
